32 devices in a mesh: dp: 4 (over x, core), fsdp: 8 (over z, y).
Axes of the slice: x: 2, y: 2, z: 4, core: 2. Of those that a mesh axis runs over, the one named last changes fastest.
Arguments:
- queries: bfloat16 [64, 128, 1280], P(('dp', 'fsdp')), may hold values from -100 to 100
- keys: bfloat16 [64, 128, 1280], P(('dp', 'fsdp')), may hold values from -100 to 100
- values: bfloat16 [64, 128, 1280], P(('dp', 'fsdp')), may hold values from -64 to 64
- block_len: int32 [64], P(('dp', 'fsdp')), may hold values from 0 to 128, as said below
- target: int32 [64], P(('dp', 'fsdp')), may hold values from 0 to 2, as said below
- cotangent: bfloat16 [32, 128, 1280], P(('dp', 'fsdp')), may hold values from -6 to 6
- out_weight: bfloat16 [1280, 1280], P('fsdp'), may hold values from -0.15625 to 0.15625
Outputs:
- embedding: bfloat16 [32, 128, 1280], P(('dp', 'fsdp'))
- weight_grad: float32 [1280, 1280], P('fsdp')
The draws below stay inside these ranges and needn't reach their ends.
Inputs may be any that keep to these rules, and one draw needn't show every extreme that they name: `block_len`: 0 exactly in the empty slots, those with target 2; live blocks hold 1 to 128 patches; in every draw some device has all its slots live and full. `target`: t < 1: output slot t of the same device; 1 <= t < 2: output slot t - 1 of the next device along dp (wrapping), same fsdp index; t = 2: empty slot; live values are distinct within a device, every output slot receives exactly one block, and in every draw some device has all 2 slots live.
All inputs are finite; a program needn't handle non-finite values.
Results may differ from the reference program's by a relative error of at most 0.012.
Values may be sent and summed in bfloat16 or wider, within the bound.
A program may use at most 64 MiB of HBM per device.

```python
import jax
import jax.numpy as jnp
from jax import lax

D = 1280
HEADS = 16
HEAD_DIM = 80
WIN = 128
OUT_DEV = 1
SLOTS = 2
IN_BLOCKS = 64
OUT_BLOCKS = 32
N_DP = 4
N_FSDP = 8
DEVICES = 32


def attention_pair(key):
    base = jax.random.fold_in(key, 101)
    key_query, key_key = jax.random.split(base, 2)
    shape = (IN_BLOCKS, WIN, HEADS, HEAD_DIM)
    query_draw = jnp.clip(jax.random.normal(key_query, shape, jnp.float32), -6.0, 6.0)
    key_draw = jnp.clip(jax.random.normal(key_key, shape, jnp.float32), -6.0, 6.0)
    return (query_draw.reshape(IN_BLOCKS, WIN, D), key_draw.reshape(IN_BLOCKS, WIN, D))


def draw_queries(key, part):
    return attention_pair(key)[0].astype(jnp.bfloat16)


def draw_keys(key, part):
    return attention_pair(key)[1].astype(jnp.bfloat16)


def draw_values(key, part):
    base = jax.random.fold_in(key, 303)
    key_noise, key_head = jax.random.split(base, 2)
    head_index = jnp.arange(HEADS, dtype=jnp.float32) / max(HEADS - 1, 1)
    jitter = jnp.exp(0.25 * jnp.clip(jax.random.normal(key_head, (HEADS,), jnp.float32), -2.0, 2.0))
    shape = (IN_BLOCKS, WIN, HEADS, HEAD_DIM)
    head_scale = 0.5 * jnp.power(3.0, head_index) * jitter
    noise = jnp.clip(jax.random.normal(key_noise, shape, jnp.float32), -6.0, 6.0)
    drawn = noise * head_scale[:, None]
    return drawn.reshape(IN_BLOCKS, WIN, D).astype(jnp.bfloat16)


def routing(key):
    base = jax.random.fold_in(key, 202)
    key_left, key_forced, key_order, key_full, key_short = jax.random.split(base, 5)
    from_left = jax.random.randint(key_left, (N_DP, N_FSDP, OUT_DEV), 0, 2)
    forced = jax.random.randint(key_forced, (), 0, N_DP)
    cycle_index = jnp.arange(N_DP, dtype=jnp.int32)[:, None, None]
    from_left = jnp.where(cycle_index == forced, 0, from_left)
    from_left = jnp.where(cycle_index == (forced + 1) % N_DP, 1, from_left)
    next_left = jnp.roll(from_left, -1, axis=0)
    occupied = jnp.concatenate([from_left == 0, next_left == 1], axis=2)
    scores = jax.random.randint(key_order, (N_DP, N_FSDP, SLOTS), 0, 1 << 20) * SLOTS + jnp.arange(SLOTS, dtype=jnp.int32)
    ordering = jnp.argsort(scores, axis=2).astype(jnp.int32)
    occupied_slot = jnp.take_along_axis(occupied, ordering, axis=2)
    full_pick = jax.random.randint(key_full, (N_DP, N_FSDP, SLOTS), 0, 4)
    short_len = jax.random.randint(key_short, (N_DP, N_FSDP, SLOTS), 1, WIN + 1)
    lengths = jnp.where(full_pick < 3, WIN, short_len)
    lengths = jnp.where(cycle_index == forced, WIN, lengths)
    target_out = jnp.where(occupied_slot, ordering, SLOTS).astype(jnp.int32).reshape(IN_BLOCKS)
    length_out = jnp.where(occupied_slot, lengths, 0).astype(jnp.int32).reshape(IN_BLOCKS)
    return (target_out, length_out)


def draw_block_len(key, part):
    return routing(key)[1]


def draw_target(key, part):
    return routing(key)[0]


def block_scale(key, shape, cuts, least, high):
    factor_of, own = 1.0, jax.random.fold_in(key, 6)
    for dim, parts in cuts:
        heights = jnp.exp(jax.random.uniform(jax.random.fold_in(own, dim), (parts,), jnp.float32, least / len(cuts), high / len(cuts)))
        factor_of = factor_of * jnp.repeat(heights, shape[dim] // parts).reshape([-1 if axis == dim else 1 for axis in range(len(shape))])
    return factor_of


def normal_values(own_key, extent, spread, limit, pieces=(), kind=jnp.bfloat16):
    result = spread * jax.random.normal(own_key, extent, jnp.float32)
    if pieces:
        result = result * block_scale(own_key, extent, pieces, -0.22, 0.18)
    return jnp.clip(result, -limit, limit).astype(kind)


def setup_inputs(seed: int = 0) -> dict:
    arg_keys = jax.random.split(jax.random.key(seed), 8)
    queries = draw_queries(jax.random.fold_in(arg_keys[7], 71), 0)
    keys = draw_keys(jax.random.fold_in(arg_keys[7], 71), 0)
    values = draw_values(jax.random.fold_in(arg_keys[7], 71), 0)
    block_len = draw_block_len(jax.random.fold_in(arg_keys[7], 71), 0)
    target = draw_target(jax.random.fold_in(arg_keys[7], 71), 0)
    cotangent = normal_values(arg_keys[5], (OUT_BLOCKS, WIN, D), 1.0, 6.0, ((0, 32),))
    out_weight = normal_values(arg_keys[6], (D, D), D ** -0.5, 0.15625, ((0, 8),))
    return {"queries": queries, "keys": keys, "values": values, "block_len": block_len, "target": target, "cotangent": cotangent, "out_weight": out_weight}


def attend_block(query, key_block, value_block, length):
    shape = (WIN, HEADS, HEAD_DIM)
    query_heads = query.reshape(shape).astype(jnp.float32)
    key_heads = key_block.reshape(shape).astype(jnp.float32)
    value_heads = value_block.reshape(shape).astype(jnp.float32)
    scores = jnp.einsum('qhd,khd->hqk', query_heads, key_heads) * HEAD_DIM ** (-0.5)
    position = jnp.arange(WIN, dtype=jnp.int32)
    usable = position < length
    scores = jnp.where(usable[None, None, :], scores, -1e+30)
    highest = lax.optimization_barrier(jnp.max(scores, axis=-1, keepdims=True))
    exponent = jnp.exp(scores - highest)
    attn_weights = (exponent / lax.optimization_barrier(jnp.sum(exponent, axis=-1, keepdims=True))).astype(jnp.bfloat16)
    mixed_out = jnp.einsum('hqk,khd->qhd', attn_weights.astype(jnp.float32), value_heads)
    mixed_out = jnp.where(usable[:, None, None], mixed_out, 0.0)
    return mixed_out.reshape(WIN, D).astype(jnp.bfloat16)

def reference(queries, keys, values, block_len, target, cotangent, out_weight):
    attended_in = lax.map(lambda item: attend_block(item[0], item[1], item[2], item[3]), (queries, keys, values, block_len))
    block_index = jnp.arange(IN_BLOCKS, dtype=jnp.int32)
    device = block_index // SLOTS
    cycle_index = device // N_FSDP
    column = device % N_FSDP
    step_over = target // OUT_DEV
    out_slot = target % OUT_DEV
    owner = (cycle_index + step_over) % N_DP
    destination = (owner * N_FSDP + column) * OUT_DEV + out_slot
    destination = jnp.where(target == SLOTS, OUT_BLOCKS, destination).astype(jnp.int32)
    placed = jnp.zeros((OUT_BLOCKS, WIN, D), jnp.bfloat16).at[destination].set(attended_in, mode='drop')
    flat_rows = placed.reshape(OUT_BLOCKS * WIN, D)
    embedding = jnp.dot(flat_rows, out_weight, preferred_element_type=jnp.float32).astype(jnp.bfloat16)
    embedding = embedding.reshape(OUT_BLOCKS, WIN, D)
    per_device = flat_rows.reshape(DEVICES, OUT_DEV * WIN, D)
    cot_device = cotangent.reshape(DEVICES, OUT_DEV * WIN, D)

    def accumulate(running, item):
        partial_grad = jnp.dot(item[0].T, item[1], preferred_element_type=jnp.float32)
        rounded = lax.optimization_barrier(partial_grad.astype(jnp.bfloat16)).astype(jnp.float32)
        return (running + rounded, None)
    raw_grad, unused = lax.scan(accumulate, jnp.zeros((D, D), jnp.float32), (per_device, cot_device))
    grad_norm = jnp.sqrt(jnp.sum(raw_grad * raw_grad) + 1e-06)
    weight_grad = raw_grad * jnp.minimum(1.0, D / grad_norm)
    return (embedding, weight_grad)
```

```python
import functools
import math

import jax
import jax.numpy as jnp
from jax import lax
from jax.experimental import pallas as pl
from jax.experimental.pallas import tpu as pltpu
from jax.sharding import PartitionSpec as P

HEADS = 16
LANES = 128
MESH = pl.DeviceIdType.MESH
F32 = jnp.float32
BF16 = jnp.bfloat16


def starts_of(width, group):
    tiles = width // LANES
    window = -(-tiles // group) * LANES
    return window, [min(i * window, width - window) for i in range(group)]


def kernel(
    n_dp, n_fs, group, finish,
    len_ref, tgt_ref, q_ref, k_ref, v_ref, cot_ref, w_ref,
    emb_ref, grad_ref,
    wq, cq, mine, nxt, arr, placed, gpart, yrecv, zsend, zrecv, esend, ebuf, tbuf, sbuf, srecv,
    wz_s, wz_r, wy_s, wy_r, c_s, c_r, n_s, n_r, p_s, p_r, gy_s, gy_r, gz_s, gz_r,
    e_s, e_r, t_s, t_r, q_s, q_r,
):
    slots, rows, width = q_ref.shape
    shard = w_ref.shape[0]
    hd = width // HEADS
    window, starts = starts_of(width, group)
    over = group * window - width
    nz = n_fs // 2
    d, f = lax.axis_index("dp"), lax.axis_index("fsdp")
    base = (d // group) * group
    gi = d - base
    z, y = f // 2, f % 2
    other = z * 2 + (1 - y)
    ahead, behind = (d + 1) % n_dp, (d + n_dp - 1) % n_dp
    mates = [(gi + j) % group for j in range(1, group)]

    def start_of(i):
        if group == 1:
            return 0
        return pl.multiple_of(i * window - (i // (group - 1)) * over, LANES)

    def copy(src, dst, s, r, to):
        return pltpu.make_async_remote_copy(
            src_ref=src, dst_ref=dst, send_sem=s, recv_sem=r, device_id=to, device_id_type=MESH
        )

    barrier = pltpu.get_barrier_semaphore()
    peers = [(ahead, f), (behind, f)]
    peers += [(base + m, f) for m in mates]
    peers += [(d, (f + j) % n_fs) for j in range(1, n_fs)]
    for peer in peers:
        pl.semaphore_signal(barrier, inc=1, device_id=peer, device_id_type=MESH)
    pl.semaphore_wait(barrier, len(peers))

    my_cols = pl.ds(start_of(gi), window)
    my_rows = pl.ds(pl.multiple_of(gi * rows, rows), rows)

    def w_at(index):
        return wq.at[pl.ds(pl.multiple_of(index * shard, shard), shard), :]

    sends = []
    w_src = w_ref.at[:, my_cols]
    wz = []
    for j in range(1, nz):
        c = copy(w_src, w_at(f), wz_s.at[j], wz_r.at[j], (d, ((z + j) % nz) * 2 + y))
        c.start()
        wz.append(c)
    wy = [copy(w_src, w_at(f), wy_s.at[0], wy_r.at[0], (d, other))]
    wy[0].start()
    cots = []
    for j, m in enumerate(mates):
        c = copy(
            cot_ref.at[0, :, pl.ds(start_of(m), window)], cq.at[my_rows, :],
            c_s.at[j], c_r.at[j], (base + m, f),
        )
        c.start()
        cots.append(c)
    wq[pl.ds(pl.multiple_of(f * shard, shard), shard), :] = w_ref[:, my_cols]
    cq[my_rows, :] = cot_ref[0, :, my_cols]

    key_pos = lax.broadcasted_iota(jnp.int32, (rows, rows), 1)
    row_pos = lax.broadcasted_iota(jnp.int32, (rows, LANES), 0)
    lens = [len_ref[s] for s in range(slots)]
    usable = [key_pos < lens[s] for s in range(slots)]
    limit = [[jnp.where(tgt_ref[s] == t, lens[s], 0) for s in range(slots)] for t in range(2)]
    keep = [[row_pos < limit[t][s] for s in range(slots)] for t in range(2)]
    tiles = {}
    half = width // 2
    nexts = []

    def send_next(part):
        cols = pl.ds(part * half, half)
        c = copy(nxt.at[:, cols], arr.at[:, cols], n_s.at[part], n_r.at[part], (ahead, f))
        c.start()
        nexts.append(c)

    for h in range(HEADS):
        first, last = h * hd, (h + 1) * hd
        lo, hi = first // LANES * LANES, -(-last // LANES) * LANES
        lane = lax.broadcasted_iota(jnp.int32, (rows, hi - lo), 1) + lo
        inside = (lane >= first) & (lane < last)
        for s in range(slots):
            query = jnp.where(inside, q_ref[s, :, lo:hi].astype(F32), 0.0).astype(BF16)
            scores = lax.dot_general(
                query, k_ref[s, :, lo:hi], (((1,), (1,)), ((), ())), preferred_element_type=F32
            ) * hd ** (-0.5)
            scores = jnp.where(usable[s], scores, -1e30)
            exponent = jnp.exp(scores - jnp.max(scores, axis=-1, keepdims=True))
            weights = (exponent / jnp.sum(exponent, axis=-1, keepdims=True)).astype(BF16)
            mixed = jnp.dot(weights, v_ref[s, :, lo:hi], preferred_element_type=F32)
            mixed = jnp.where(inside, mixed, 0.0)
            for t in range(lo // LANES, hi // LANES):
                piece = mixed[:, t * LANES - lo:(t + 1) * LANES - lo]
                tiles[s, t] = tiles[s, t] + piece if (s, t) in tiles else piece
        for t in range(lo // LANES, hi // LANES):
            if (t + 1) * LANES <= last:
                cols = slice(t * LANES, (t + 1) * LANES)
                for dest, ref in ((0, mine), (1, nxt)):
                    total = sum(
                        jnp.where(keep[dest][s], tiles[s, t], 0.0) for s in range(slots)
                    )
                    ref[:, cols] = total.astype(BF16)
        if last == half:
            send_next(0)
    send_next(1)

    for j in range(1, nz):
        wz[j - 1].wait_recv()
        from_f = ((z + nz - j) % nz) * 2 + y
        c = copy(w_at(from_f), w_at(from_f), wy_s.at[j], wy_r.at[j], (d, other))
        c.start()
        wy.append(c)

    casts = []
    for part in range(2):
        nexts[part].wait_recv()
        cols = pl.ds(part * half, half)
        placed[my_rows, cols] = mine[:, cols] + arr[:, cols]
        for j, m in enumerate(mates):
            c = copy(
                placed.at[my_rows, cols], placed.at[my_rows, cols],
                p_s.at[part, j], p_r.at[part, j], (base + m, f),
            )
            c.start()
            casts.append(c)
    for c in cots + casts:
        c.wait_recv()

    step = 2 * LANES
    for i in range(width // step):
        gpart[i * step:(i + 1) * step, :] = lax.dot_general(
            placed[:, i * step:(i + 1) * step], cq[...], (((0,), (0,)), ((), ())),
            preferred_element_type=F32,
        ).astype(BF16)

    def g_rows(index):
        return pl.ds(pl.multiple_of(index * shard, shard), shard)

    order = list(range(1, nz)) + [0]
    gy = []
    for j in order:
        zj = (z + j) % nz
        c = copy(
            gpart.at[g_rows(zj * 2 + (1 - y)), :], yrecv.at[zj],
            gy_s.at[j], gy_r.at[j], (d, other),
        )
        c.start()
        gy.append(c)
    gz = []
    for j, c in zip(order, gy):
        zj = (z + j) % nz
        c.wait_recv()
        pair = gpart[g_rows(zj * 2 + y), :].astype(F32) + yrecv[zj].astype(F32)
        if j == 0:
            own = pair
        else:
            zsend[j] = pair.astype(BF16)
            c = copy(zsend.at[j], zrecv.at[j], gz_s.at[j], gz_r.at[j], (d, zj * 2 + y))
            c.start()
            gz.append(c)

    for c in wy:
        c.wait_recv()
    embs = []
    for i in range(group):
        esend[i] = jnp.dot(
            placed[i * rows:(i + 1) * rows, :], wq[...], preferred_element_type=F32
        ).astype(BF16)
    for j, m in enumerate(mates):
        c = copy(esend.at[m], ebuf.at[gi], e_s.at[j], e_r.at[j], (base + m, f))
        c.start()
        embs.append(c)
    ebuf[gi] = esend[gi]

    for c in gz:
        c.wait_recv()
    for j in range(1, nz):
        own = own + zrecv[j].astype(F32)
    tbuf[gi] = own.astype(BF16)
    turns = []
    for j, m in enumerate(mates):
        c = copy(tbuf.at[gi], tbuf.at[gi], t_s.at[j], t_r.at[j], (base + m, f))
        c.start()
        turns.append(c)
    for c in embs:
        c.wait_recv()
    ends = starts[1:] + [width]
    for i in range(group):
        emb_ref[0, :, starts[i]:ends[i]] = ebuf[i, :, 0:ends[i] - starts[i]]
    for c in turns:
        c.wait_recv()
    squares = []
    if finish:
        total = jnp.zeros((8, LANES), F32)
        for i in range(group):
            for col in range(0, ends[i] - starts[i], LANES):
                tile = tbuf[i, :, col:col + LANES].astype(F32)
                total = total + jnp.sum((tile * tile).reshape(shard // 8, 8, LANES), axis=0)
        sbuf[...] = total
        for j in range(1, n_fs):
            c = copy(sbuf, srecv.at[j], q_s.at[j], q_r.at[j], (d, (f + j) % n_fs))
            c.start()
            squares.append(c)
        for c in squares:
            c.wait_recv()
        for j in range(1, n_fs):
            total = total + srecv[j]
        norm = jnp.sqrt(jnp.sum(total, keepdims=True) + 1e-06)
        factor = jnp.minimum(1.0, float(width) / norm)
    for i in range(group):
        tile = tbuf[i, :, 0:ends[i] - starts[i]].astype(F32)
        grad_ref[:, starts[i]:ends[i]] = tile * factor if finish else tile
    for c in wz + wy + cots + nexts + casts + gy + gz + embs + turns + squares:
        c.wait_send()


def local(n_dp, n_fs, group, queries, keys, values, block_len, target, cotangent, out_weight):
    slots, rows, width = queries.shape
    shard = out_weight.shape[0]
    window, starts = starts_of(width, group)
    nz = n_fs // 2
    finish = group == n_dp
    vmem = pl.BlockSpec(memory_space=pltpu.VMEM)
    smem = pl.BlockSpec(memory_space=pltpu.SMEM)
    sem = lambda *shape: pltpu.SemaphoreType.DMA(shape)
    mates = max(group - 1, 1)
    embedding, grad = pl.pallas_call(
        functools.partial(kernel, n_dp, n_fs, group, finish),
        out_shape=(
            jax.ShapeDtypeStruct(cotangent.shape, BF16),
            jax.ShapeDtypeStruct((shard, width), F32),
        ),
        in_specs=[smem, smem] + [vmem] * 5,
        out_specs=(vmem, vmem),
        scratch_shapes=[
            pltpu.VMEM((width, window), BF16),
            pltpu.VMEM((group * rows, window), BF16),
            pltpu.VMEM((rows, width), BF16),
            pltpu.VMEM((rows, width), BF16),
            pltpu.VMEM((rows, width), BF16),
            pltpu.VMEM((group * rows, width), BF16),
            pltpu.VMEM((width, window), BF16),
            pltpu.VMEM((nz, shard, window), BF16),
            pltpu.VMEM((nz, shard, window), BF16),
            pltpu.VMEM((nz, shard, window), BF16),
            pltpu.VMEM((group, rows, window), BF16),
            pltpu.VMEM((group, rows, window), BF16),
            pltpu.VMEM((group, shard, window), BF16),
            pltpu.VMEM((8, LANES), F32),
            pltpu.VMEM((n_fs, 8, LANES), F32),
            sem(nz), sem(nz), sem(nz), sem(nz), sem(mates), sem(mates), sem(2), sem(2),
            sem(2, mates), sem(2, mates), sem(nz), sem(nz), sem(nz), sem(nz),
            sem(mates), sem(mates), sem(mates), sem(mates), sem(n_fs), sem(n_fs),
        ],
        compiler_params=pltpu.CompilerParams(collective_id=0, has_side_effects=True),
    )(block_len, target, queries, keys, values, cotangent, out_weight)
    if not finish:
        lines = [[i for i in range(n_dp) if i % group == g] for g in range(group)]
        grad = lax.psum(grad, "dp", axis_index_groups=lines)
        squares = lax.psum(jnp.sum(grad * grad), "fsdp")
        grad = grad * jnp.minimum(1.0, float(width) / jnp.sqrt(squares + 1e-06))
    return embedding, grad


def solution(mesh):
    n_dp, n_fs = mesh.shape["dp"], mesh.shape["fsdp"]
    group = math.gcd(n_dp, 4)
    both = P(("dp", "fsdp"), None, None)
    flat = P(("dp", "fsdp"))
    return jax.shard_map(
        functools.partial(local, n_dp, n_fs, group),
        mesh=mesh,
        in_specs=(both, both, both, flat, flat, both, P("fsdp", None)),
        out_specs=(both, P("fsdp", None)),
        check_vma=False,
    )
```

```python
import functools
import math

import jax
import jax.numpy as jnp
from jax import lax
from jax.experimental import pallas as pl
from jax.experimental.pallas import tpu as pltpu
from jax.sharding import PartitionSpec as P

HEADS = 16
LANES = 128
MESH = pl.DeviceIdType.MESH
F32 = jnp.float32
BF16 = jnp.bfloat16


def starts_of(width, group):
    tiles = width // LANES
    window = -(-tiles // group) * LANES
    return window, [min(i * window, width - window) for i in range(group)]


def kernel(
    n_dp, n_fs, group, finish,
    len_ref, tgt_ref, q_ref, k_ref, v_ref, cot_ref, w_ref,
    emb_ref, grad_ref,
    wq, cq, mine, nxt, arr, placed, gpart, yrecv, zsend, zrecv, esend, ebuf, tbuf, sbuf, srecv, gsum,
    wz_s, wz_r, wy_s, wy_r, c_s, c_r, n_s, n_r, p_s, p_r, gy_s, gy_r, gz_s, gz_r,
    e_s, e_r, t_s, t_r, q_s, q_r, m_s, m_r,
):
    slots, rows, width = q_ref.shape
    shard = w_ref.shape[0]
    hd = width // HEADS
    window, starts = starts_of(width, group)
    over = group * window - width
    nz = n_fs // 2
    d, f = lax.axis_index("dp"), lax.axis_index("fsdp")
    base = (d // group) * group
    gi = d - base
    z, y = f // 2, f % 2
    other = z * 2 + (1 - y)
    ahead, behind = (d + 1) % n_dp, (d + n_dp - 1) % n_dp
    mates = [(gi + j) % group for j in range(1, group)]
    core, side = gi % 2, gi // 2
    partner, across = side * 2 + (1 - core), (1 - side) * 2 + core

    def start_of(i):
        if group == 1:
            return 0
        return pl.multiple_of(i * window - (i // (group - 1)) * over, LANES)

    def copy(src, dst, s, r, to):
        return pltpu.make_async_remote_copy(
            src_ref=src, dst_ref=dst, send_sem=s, recv_sem=r, device_id=to, device_id_type=MESH
        )

    def spread(at, s, r):
        to = [partner, across] if group == 4 else mates
        made = [copy(at(gi), at(gi), s(j), r(j), (base + m, f)) for j, m in enumerate(to)]
        for c in made:
            c.start()
        return made

    def relay(made, at, s, r):
        if group != 4:
            return made
        made[1].wait_recv()
        c = copy(at(across), at(across), s(2), r(2), (base + partner, f))
        c.start()
        made.append(c)
        return [made[0], c]

    barrier = pltpu.get_barrier_semaphore()
    peers = [(ahead, f), (behind, f)]
    peers += [(base + m, f) for m in mates]
    peers += [(d, (f + j) % n_fs) for j in range(1, n_fs)]
    for peer in peers:
        pl.semaphore_signal(barrier, inc=1, device_id=peer, device_id_type=MESH)
    pl.semaphore_wait(barrier, len(peers))

    my_cols = pl.ds(start_of(gi), window)
    my_rows = pl.ds(pl.multiple_of(gi * rows, rows), rows)

    def w_at(index):
        return wq.at[pl.ds(pl.multiple_of(index * shard, shard), shard), :]

    sends = []
    w_src = w_ref.at[:, my_cols]
    wz = []
    for j in range(1, nz):
        c = copy(w_src, w_at(f), wz_s.at[j], wz_r.at[j], (d, ((z + j) % nz) * 2 + y))
        c.start()
        wz.append(c)
    wy = [copy(w_src, w_at(f), wy_s.at[0], wy_r.at[0], (d, other))]
    wy[0].start()
    cots = []
    for j, m in enumerate(mates):
        c = copy(
            cot_ref.at[0, :, pl.ds(start_of(m), window)], cq.at[my_rows, :],
            c_s.at[j], c_r.at[j], (base + m, f),
        )
        c.start()
        cots.append(c)
    wq[pl.ds(pl.multiple_of(f * shard, shard), shard), :] = w_ref[:, my_cols]
    cq[my_rows, :] = cot_ref[0, :, my_cols]

    key_pos = lax.broadcasted_iota(jnp.int32, (rows, rows), 1)
    row_pos = lax.broadcasted_iota(jnp.int32, (rows, LANES), 0)
    lens = [len_ref[s] for s in range(slots)]
    usable = [key_pos < lens[s] for s in range(slots)]
    limit = [[jnp.where(tgt_ref[s] == t, lens[s], 0) for s in range(slots)] for t in range(2)]
    keep = [[row_pos < limit[t][s] for s in range(slots)] for t in range(2)]
    tiles = {}
    half = width // 2
    nexts = []

    def send_next(part):
        cols = pl.ds(part * half, half)
        c = copy(nxt.at[:, cols], arr.at[:, cols], n_s.at[part], n_r.at[part], (ahead, f))
        c.start()
        nexts.append(c)

    def placed_at(part):
        cols = pl.ds(part * half, half)
        return lambda i: placed.at[pl.ds(pl.multiple_of(i * rows, rows), rows), cols]

    def cast(part):
        nexts[part].wait_recv()
        cols = pl.ds(part * half, half)
        placed[my_rows, cols] = mine[:, cols] + arr[:, cols]
        return spread(placed_at(part), lambda j: p_s.at[part, j], lambda j: p_r.at[part, j])

    def hand_on(part, made):
        return relay(
            made, placed_at(part), lambda j: p_s.at[part, j], lambda j: p_r.at[part, j]
        )

    for h in range(HEADS):
        first, last = h * hd, (h + 1) * hd
        lo, hi = first // LANES * LANES, -(-last // LANES) * LANES
        lane = lax.broadcasted_iota(jnp.int32, (rows, hi - lo), 1) + lo
        inside = (lane >= first) & (lane < last)
        for s in range(slots):
            query = jnp.where(inside, q_ref[s, :, lo:hi].astype(F32), 0.0).astype(BF16)
            scores = lax.dot_general(
                query, k_ref[s, :, lo:hi], (((1,), (1,)), ((), ())), preferred_element_type=F32
            ) * hd ** (-0.5)
            scores = jnp.where(usable[s], scores, -1e30)
            exponent = jnp.exp(scores - jnp.max(scores, axis=-1, keepdims=True))
            weights = (exponent / jnp.sum(exponent, axis=-1, keepdims=True)).astype(BF16)
            mixed = jnp.dot(weights, v_ref[s, :, lo:hi], preferred_element_type=F32)
            mixed = jnp.where(inside, mixed, 0.0)
            for t in range(lo // LANES, hi // LANES):
                piece = mixed[:, t * LANES - lo:(t + 1) * LANES - lo]
                tiles[s, t] = tiles[s, t] + piece if (s, t) in tiles else piece
        for t in range(lo // LANES, hi // LANES):
            if (t + 1) * LANES <= last:
                cols = slice(t * LANES, (t + 1) * LANES)
                for dest, ref in ((0, mine), (1, nxt)):
                    total = sum(
                        jnp.where(keep[dest][s], tiles[s, t], 0.0) for s in range(slots)
                    )
                    ref[:, cols] = total.astype(BF16)
        if last == half:
            send_next(0)
        if h == HEADS * 3 // 4 - 1:
            cast0 = cast(0)
    send_next(1)
    waits = hand_on(0, cast0)
    cast1 = cast(1)

    for j in range(1, nz):
        wz[j - 1].wait_recv()
        from_f = ((z + nz - j) % nz) * 2 + y
        c = copy(w_at(from_f), w_at(from_f), wy_s.at[j], wy_r.at[j], (d, other))
        c.start()
        wy.append(c)

    waits += hand_on(1, cast1)
    casts = cast0 + cast1
    for c in cots + waits:
        c.wait_recv()

    step = 2 * LANES
    for i in range(width // step):
        gpart[i * step:(i + 1) * step, :] = lax.dot_general(
            placed[:, i * step:(i + 1) * step], cq[...], (((0,), (0,)), ((), ())),
            preferred_element_type=F32,
        ).astype(BF16)

    def g_rows(index):
        return pl.ds(pl.multiple_of(index * shard, shard), shard)

    order = list(range(1, nz)) + [0]
    gy = []
    for j in order:
        zj = (z + j) % nz
        c = copy(
            gpart.at[g_rows(zj * 2 + (1 - y)), :], yrecv.at[zj],
            gy_s.at[j], gy_r.at[j], (d, other),
        )
        c.start()
        gy.append(c)
    gz = []
    for j, c in zip(order, gy):
        zj = (z + j) % nz
        c.wait_recv()
        pair = gpart[g_rows(zj * 2 + y), :].astype(F32) + yrecv[zj].astype(F32)
        if j == 0:
            own = pair
        else:
            zsend[j] = pair.astype(BF16)
            c = copy(zsend.at[j], zrecv.at[j], gz_s.at[j], gz_r.at[j], (d, zj * 2 + y))
            c.start()
            gz.append(c)

    for c in wy:
        c.wait_recv()
    embs = []
    for i in range(group):
        esend[i] = jnp.dot(
            placed[i * rows:(i + 1) * rows, :], wq[...], preferred_element_type=F32
        ).astype(BF16)
    for j, m in enumerate(mates):
        c = copy(esend.at[m], ebuf.at[gi], e_s.at[j], e_r.at[j], (base + m, f))
        c.start()
        embs.append(c)
    ebuf[gi] = esend[gi]

    for c in gz:
        c.wait_recv()
    for j in range(1, nz):
        own = own + zrecv[j].astype(F32)
    ends = starts[1:] + [width]
    tbuf[gi] = own.astype(BF16)
    turn_at = lambda i: tbuf.at[i]
    turn_s, turn_r = (lambda j: t_s.at[j]), (lambda j: t_r.at[j])
    turns = spread(turn_at, turn_s, turn_r)
    squares = []
    if finish:
        valid = window
        for i in range(group):
            valid = jnp.where(gi == i, ends[i] - starts[i], valid)
        lane = lax.broadcasted_iota(jnp.int32, (8, LANES), 1)
        total = jnp.zeros((8, LANES), F32)
        for col in range(0, window, LANES):
            tile = own[:, col:col + LANES].astype(BF16).astype(F32)
            part = jnp.sum((tile * tile).reshape(shard // 8, 8, LANES), axis=0)
            total = total + jnp.where(lane + col < valid, part, 0.0)
        sbuf[...] = total
        for j in range(1, n_fs):
            c = copy(sbuf, srecv.at[j], q_s.at[j], q_r.at[j], (d, (f + j) % n_fs))
            c.start()
            squares.append(c)
    waits = relay(turns, turn_at, turn_s, turn_r)
    if finish:
        for j, c in zip(range(1, n_fs), squares):
            c.wait_recv()
            total = total + srecv[j]
        gsum[gi] = total
        for j, m in enumerate(mates):
            c = copy(gsum.at[gi], gsum.at[gi], m_s.at[j], m_r.at[j], (base + m, f))
            c.start()
            squares.append(c)
    for c in embs:
        c.wait_recv()
    for i in range(group):
        emb_ref[0, :, starts[i]:ends[i]] = ebuf[i, :, 0:ends[i] - starts[i]]
    for c in waits:
        c.wait_recv()
    if finish:
        for c in squares[n_fs - 1:]:
            c.wait_recv()
        total = gsum[0]
        for i in range(1, group):
            total = total + gsum[i]
        norm = jnp.sqrt(jnp.sum(total, keepdims=True) + 1e-06)
        factor = jnp.minimum(1.0, float(width) / norm)
    for i in range(group):
        tile = tbuf[i, :, 0:ends[i] - starts[i]].astype(F32)
        grad_ref[:, starts[i]:ends[i]] = tile * factor if finish else tile
    for c in wz + wy + cots + nexts + casts + gy + gz + embs + turns + squares:
        c.wait_send()


def local(n_dp, n_fs, group, queries, keys, values, block_len, target, cotangent, out_weight):
    slots, rows, width = queries.shape
    shard = out_weight.shape[0]
    window, starts = starts_of(width, group)
    nz = n_fs // 2
    finish = group == n_dp
    vmem = pl.BlockSpec(memory_space=pltpu.VMEM)
    smem = pl.BlockSpec(memory_space=pltpu.SMEM)
    sem = lambda *shape: pltpu.SemaphoreType.DMA(shape)
    mates = max(group - 1, 1)
    embedding, grad = pl.pallas_call(
        functools.partial(kernel, n_dp, n_fs, group, finish),
        out_shape=(
            jax.ShapeDtypeStruct(cotangent.shape, BF16),
            jax.ShapeDtypeStruct((shard, width), F32),
        ),
        in_specs=[smem, smem] + [vmem] * 5,
        out_specs=(vmem, vmem),
        scratch_shapes=[
            pltpu.VMEM((width, window), BF16),
            pltpu.VMEM((group * rows, window), BF16),
            pltpu.VMEM((rows, width), BF16),
            pltpu.VMEM((rows, width), BF16),
            pltpu.VMEM((rows, width), BF16),
            pltpu.VMEM((group * rows, width), BF16),
            pltpu.VMEM((width, window), BF16),
            pltpu.VMEM((nz, shard, window), BF16),
            pltpu.VMEM((nz, shard, window), BF16),
            pltpu.VMEM((nz, shard, window), BF16),
            pltpu.VMEM((group, rows, window), BF16),
            pltpu.VMEM((group, rows, window), BF16),
            pltpu.VMEM((group, shard, window), BF16),
            pltpu.VMEM((8, LANES), F32),
            pltpu.VMEM((n_fs, 8, LANES), F32),
            pltpu.VMEM((group, 8, LANES), F32),
            sem(nz), sem(nz), sem(nz), sem(nz), sem(mates), sem(mates), sem(2), sem(2),
            sem(2, mates), sem(2, mates), sem(nz), sem(nz), sem(nz), sem(nz),
            sem(mates), sem(mates), sem(mates), sem(mates), sem(n_fs), sem(n_fs),
            sem(mates), sem(mates),
        ],
        compiler_params=pltpu.CompilerParams(collective_id=0, has_side_effects=True),
    )(block_len, target, queries, keys, values, cotangent, out_weight)
    if not finish:
        lines = [[i for i in range(n_dp) if i % group == g] for g in range(group)]
        grad = lax.psum(grad, "dp", axis_index_groups=lines)
        squares = lax.psum(jnp.sum(grad * grad), "fsdp")
        grad = grad * jnp.minimum(1.0, float(width) / jnp.sqrt(squares + 1e-06))
    return embedding, grad


def solution(mesh):
    n_dp, n_fs = mesh.shape["dp"], mesh.shape["fsdp"]
    group = math.gcd(n_dp, 4)
    both = P(("dp", "fsdp"), None, None)
    flat = P(("dp", "fsdp"))
    return jax.shard_map(
        functools.partial(local, n_dp, n_fs, group),
        mesh=mesh,
        in_specs=(both, both, both, flat, flat, both, P("fsdp", None)),
        out_specs=(both, P("fsdp", None)),
        check_vma=False,
    )
```

```python
import functools
import math

import jax
import jax.numpy as jnp
from jax import lax
from jax.experimental import pallas as pl
from jax.experimental.pallas import tpu as pltpu
from jax.sharding import PartitionSpec as P

HEADS = 16
LANES = 128
MESH = pl.DeviceIdType.MESH
F32 = jnp.float32
BF16 = jnp.bfloat16


def starts_of(width, group):
    tiles = width // LANES
    window = -(-tiles // group) * LANES
    return window, [min(i * window, width - window) for i in range(group)]


def marks_of(width):
    tiles = width // LANES
    return [tiles * tenths // 10 * LANES for tenths in (0, 4, 7, 9, 10)]


def kernel(
    n_dp, n_fs, group, finish,
    len_ref, tgt_ref, q_ref, k_ref, v_ref, cot_ref, w_ref,
    emb_ref, grad_ref, factor_ref,
    wq, cq, mine, nxt, arr, placed, gpart, yrecv, zsend, zrecv, esend, ebuf, tbuf, sbuf, srecv, gsum,
    wz_s, wz_r, wy_s, wy_r, c_s, c_r, n_s, n_r, p_s, p_r, gy_s, gy_r, gz_s, gz_r,
    e_s, e_r, t_s, t_r, q_s, q_r, m_s, m_r,
):
    slots, rows, width = q_ref.shape
    shard = w_ref.shape[0]
    hd = width // HEADS
    window, starts = starts_of(width, group)
    over = group * window - width
    nz = n_fs // 2
    d, f = lax.axis_index("dp"), lax.axis_index("fsdp")
    base = (d // group) * group
    gi = d - base
    z, y = f // 2, f % 2
    other = z * 2 + (1 - y)
    ahead, behind = (d + 1) % n_dp, (d + n_dp - 1) % n_dp
    mates = [(gi + j) % group for j in range(1, group)]
    core, side = gi % 2, gi // 2
    partner, across = side * 2 + (1 - core), (1 - side) * 2 + core

    def start_of(i):
        if group == 1:
            return 0
        return pl.multiple_of(i * window - (i // (group - 1)) * over, LANES)

    def copy(src, dst, s, r, to):
        return pltpu.make_async_remote_copy(
            src_ref=src, dst_ref=dst, send_sem=s, recv_sem=r, device_id=to, device_id_type=MESH
        )

    def spread(at, s, r):
        to = [partner, across] if group == 4 else mates
        made = [copy(at(gi), at(gi), s(j), r(j), (base + m, f)) for j, m in enumerate(to)]
        for c in made:
            c.start()
        return made

    def relay(made, at, s, r):
        if group != 4:
            return made
        made[1].wait_recv()
        c = copy(at(across), at(across), s(2), r(2), (base + partner, f))
        c.start()
        made.append(c)
        return [made[0], c]

    barrier = pltpu.get_barrier_semaphore()
    peers = [(ahead, f), (behind, f)]
    peers += [(base + m, f) for m in mates]
    peers += [(d, (f + j) % n_fs) for j in range(1, n_fs)]
    for peer in peers:
        pl.semaphore_signal(barrier, inc=1, device_id=peer, device_id_type=MESH)

    my_cols = pl.ds(start_of(gi), window)
    my_rows = pl.ds(pl.multiple_of(gi * rows, rows), rows)

    def w_at(index):
        return wq.at[pl.ds(pl.multiple_of(index * shard, shard), shard), :]

    wz, wy, cots = [], [], []

    def open_links():
        pl.semaphore_wait(barrier, len(peers))
        w_src = w_ref.at[:, my_cols]
        for j in range(1, nz):
            c = copy(w_src, w_at(f), wz_s.at[j], wz_r.at[j], (d, ((z + j) % nz) * 2 + y))
            c.start()
            wz.append(c)
        wy.append(copy(w_src, w_at(f), wy_s.at[0], wy_r.at[0], (d, other)))
        wy[0].start()
        for j, m in enumerate(mates):
            c = copy(
                cot_ref.at[0, :, pl.ds(start_of(m), window)], cq.at[my_rows, :],
                c_s.at[j], c_r.at[j], (base + m, f),
            )
            c.start()
            cots.append(c)
        wq[pl.ds(pl.multiple_of(f * shard, shard), shard), :] = w_ref[:, my_cols]
        cq[my_rows, :] = cot_ref[0, :, my_cols]

    key_pos = lax.broadcasted_iota(jnp.int32, (rows, rows), 1)
    row_pos = lax.broadcasted_iota(jnp.int32, (rows, LANES), 0)
    lens = [len_ref[s] for s in range(slots)]
    usable = [key_pos < lens[s] for s in range(slots)]
    limit = [[jnp.where(tgt_ref[s] == t, lens[s], 0) for s in range(slots)] for t in range(2)]
    keep = [[row_pos < limit[t][s] for s in range(slots)] for t in range(2)]
    tiles = {}
    marks = marks_of(width)
    parts = len(marks) - 1
    nexts, cast_all = [], []

    def send_next(part):
        cols = pl.ds(marks[part], marks[part + 1] - marks[part])
        c = copy(nxt.at[:, cols], arr.at[:, cols], n_s.at[part], n_r.at[part], (ahead, f))
        c.start()
        nexts.append(c)

    def placed_at(part):
        cols = pl.ds(marks[part], marks[part + 1] - marks[part])
        return lambda i: placed.at[pl.ds(pl.multiple_of(i * rows, rows), rows), cols]

    def cast(part):
        nexts[part].wait_recv()
        cols = pl.ds(marks[part], marks[part + 1] - marks[part])
        placed[my_rows, cols] = mine[:, cols] + arr[:, cols]
        return spread(placed_at(part), lambda j: p_s.at[part, j], lambda j: p_r.at[part, j])

    def hand_on(part, made):
        return relay(
            made, placed_at(part), lambda j: p_s.at[part, j], lambda j: p_r.at[part, j]
        )

    for h in range(HEADS):
        first, last = h * hd, (h + 1) * hd
        lo, hi = first // LANES * LANES, -(-last // LANES) * LANES
        lane = lax.broadcasted_iota(jnp.int32, (rows, hi - lo), 1) + lo
        inside = (lane >= first) & (lane < last)
        for s in range(slots):
            query = jnp.where(inside, q_ref[s, :, lo:hi].astype(F32), 0.0).astype(BF16)
            scores = lax.dot_general(
                query, k_ref[s, :, lo:hi], (((1,), (1,)), ((), ())), preferred_element_type=F32
            ) * hd ** (-0.5)
            scores = jnp.where(usable[s], scores, -1e30)
            exponent = jnp.exp(scores - jnp.max(scores, axis=-1, keepdims=True))
            weights = (exponent / jnp.sum(exponent, axis=-1, keepdims=True)).astype(BF16)
            mixed = jnp.dot(weights, v_ref[s, :, lo:hi], preferred_element_type=F32)
            mixed = jnp.where(inside, mixed, 0.0)
            for t in range(lo // LANES, hi // LANES):
                piece = mixed[:, t * LANES - lo:(t + 1) * LANES - lo]
                tiles[s, t] = tiles[s, t] + piece if (s, t) in tiles else piece
        for t in range(lo // LANES, hi // LANES):
            if (t + 1) * LANES <= last:
                cols = slice(t * LANES, (t + 1) * LANES)
                for dest, ref in ((0, mine), (1, nxt)):
                    total = sum(
                        jnp.where(keep[dest][s], tiles[s, t], 0.0) for s in range(slots)
                    )
                    ref[:, cols] = total.astype(BF16)
        if h == HEADS // 8 - 1:
            open_links()
        ready = last // LANES * LANES
        while len(nexts) < parts - 1 and marks[len(nexts) + 1] <= ready:
            send_next(len(nexts))
            if len(nexts) > 1:
                cast_all.append(cast(len(nexts) - 2))
    send_next(parts - 1)
    cast_all.append(cast(parts - 2))
    waits = hand_on(0, cast_all[0])
    cast_all.append(cast(parts - 1))
    for j in range(1, nz):
        wz[j - 1].wait_recv()
        from_f = ((z + nz - j) % nz) * 2 + y
        c = copy(w_at(from_f), w_at(from_f), wy_s.at[j], wy_r.at[j], (d, other))
        c.start()
        wy.append(c)

    for part in range(1, parts):
        waits += hand_on(part, cast_all[part])
    casts = sum(cast_all, [])
    for c in cots + waits:
        c.wait_recv()

    step = 2 * LANES
    for i in range(width // step):
        gpart[i * step:(i + 1) * step, :] = lax.dot_general(
            placed[:, i * step:(i + 1) * step], cq[...], (((0,), (0,)), ((), ())),
            preferred_element_type=F32,
        ).astype(BF16)

    def g_rows(index):
        return pl.ds(pl.multiple_of(index * shard, shard), shard)

    order = list(range(1, nz)) + [0]
    gy = []
    for j in order:
        zj = (z + j) % nz
        c = copy(
            gpart.at[g_rows(zj * 2 + (1 - y)), :], yrecv.at[zj],
            gy_s.at[j], gy_r.at[j], (d, other),
        )
        c.start()
        gy.append(c)
    gz = []
    for j, c in zip(order, gy):
        zj = (z + j) % nz
        c.wait_recv()
        pair = gpart[g_rows(zj * 2 + y), :].astype(F32) + yrecv[zj].astype(F32)
        if j == 0:
            own = pair
        else:
            zsend[j] = pair.astype(BF16)
            c = copy(zsend.at[j], zrecv.at[j], gz_s.at[j], gz_r.at[j], (d, zj * 2 + y))
            c.start()
            gz.append(c)

    for c in wy:
        c.wait_recv()
    embs = []
    for i in range(group):
        esend[i] = jnp.dot(
            placed[i * rows:(i + 1) * rows, :], wq[...], preferred_element_type=F32
        ).astype(BF16)
    for j, m in enumerate(mates):
        c = copy(esend.at[m], ebuf.at[gi], e_s.at[j], e_r.at[j], (base + m, f))
        c.start()
        embs.append(c)
    ebuf[gi] = esend[gi]

    for c in gz:
        c.wait_recv()
    for j in range(1, nz):
        own = own + zrecv[j].astype(F32)
    ends = starts[1:] + [width]
    tbuf[gi] = own.astype(BF16)
    turn_at = lambda i: tbuf.at[i]
    turn_s, turn_r = (lambda j: t_s.at[j]), (lambda j: t_r.at[j])
    turns = spread(turn_at, turn_s, turn_r)
    squares = []
    if finish:
        valid = window
        for i in range(group):
            valid = jnp.where(gi == i, ends[i] - starts[i], valid)
        lane = lax.broadcasted_iota(jnp.int32, (8, LANES), 1)
        total = jnp.zeros((8, LANES), F32)
        for col in range(0, window, LANES):
            tile = own[:, col:col + LANES].astype(BF16).astype(F32)
            part = jnp.sum((tile * tile).reshape(shard // 8, 8, LANES), axis=0)
            total = total + jnp.where(lane + col < valid, part, 0.0)
        sbuf[...] = total
        for j in range(1, n_fs):
            c = copy(sbuf, srecv.at[j], q_s.at[j], q_r.at[j], (d, (f + j) % n_fs))
            c.start()
            squares.append(c)
    waits = relay(turns, turn_at, turn_s, turn_r)
    if finish:
        for j, c in zip(range(1, n_fs), squares):
            c.wait_recv()
            total = total + srecv[j]
        gsum[gi] = total
        for j, m in enumerate(mates):
            c = copy(gsum.at[gi], gsum.at[gi], m_s.at[j], m_r.at[j], (base + m, f))
            c.start()
            squares.append(c)
    for c in embs:
        c.wait_recv()
    for i in range(group):
        emb_ref[0, :, starts[i]:ends[i]] = ebuf[i, :, 0:ends[i] - starts[i]]
    for c in waits:
        c.wait_recv()
    if finish:
        for c in squares[n_fs - 1:]:
            c.wait_recv()
        total = gsum[0]
        for i in range(1, group):
            total = total + gsum[i]
        norm = jnp.sqrt(jnp.sum(total, keepdims=True) + 1e-06)
        factor = jnp.minimum(1.0, float(width) / norm)
    for i in range(group):
        grad_ref[:, starts[i]:ends[i]] = tbuf[i, :, 0:ends[i] - starts[i]]
    factor_ref[...] = jnp.broadcast_to(factor, factor_ref.shape) if finish else jnp.ones_like(factor_ref)
    for c in wz + wy + cots + nexts + casts + gy + gz + embs + turns + squares:
        c.wait_send()


def settle(emb_ref, rows_ref, factor_ref, emb_out, grad_out):
    emb_out[...] = emb_ref[...]
    grad_out[...] = rows_ref[...].astype(F32) * factor_ref[0:1, 0:1]


def local(n_dp, n_fs, group, queries, keys, values, block_len, target, cotangent, out_weight):
    slots, rows, width = queries.shape
    shard = out_weight.shape[0]
    window, starts = starts_of(width, group)
    nz = n_fs // 2
    finish = group == n_dp
    vmem = pl.BlockSpec(memory_space=pltpu.VMEM)
    smem = pl.BlockSpec(memory_space=pltpu.SMEM)
    sem = lambda *shape: pltpu.SemaphoreType.DMA(shape)
    mates = max(group - 1, 1)
    parts = len(marks_of(width)) - 1
    embedding, rows_sum, factor = pl.pallas_call(
        functools.partial(kernel, n_dp, n_fs, group, finish),
        out_shape=(
            jax.ShapeDtypeStruct(cotangent.shape, BF16),
            jax.ShapeDtypeStruct((shard, width), BF16),
            jax.ShapeDtypeStruct((8, LANES), F32),
        ),
        in_specs=[smem, smem] + [vmem] * 5,
        out_specs=(vmem, vmem, vmem),
        scratch_shapes=[
            pltpu.VMEM((width, window), BF16),
            pltpu.VMEM((group * rows, window), BF16),
            pltpu.VMEM((rows, width), BF16),
            pltpu.VMEM((rows, width), BF16),
            pltpu.VMEM((rows, width), BF16),
            pltpu.VMEM((group * rows, width), BF16),
            pltpu.VMEM((width, window), BF16),
            pltpu.VMEM((nz, shard, window), BF16),
            pltpu.VMEM((nz, shard, window), BF16),
            pltpu.VMEM((nz, shard, window), BF16),
            pltpu.VMEM((group, rows, window), BF16),
            pltpu.VMEM((group, rows, window), BF16),
            pltpu.VMEM((group, shard, window), BF16),
            pltpu.VMEM((8, LANES), F32),
            pltpu.VMEM((n_fs, 8, LANES), F32),
            pltpu.VMEM((group, 8, LANES), F32),
            sem(nz), sem(nz), sem(nz), sem(nz), sem(mates), sem(mates), sem(parts), sem(parts),
            sem(parts, mates), sem(parts, mates), sem(nz), sem(nz), sem(nz), sem(nz),
            sem(mates), sem(mates), sem(mates), sem(mates), sem(n_fs), sem(n_fs),
            sem(mates), sem(mates),
        ],
        compiler_params=pltpu.CompilerParams(collective_id=0, has_side_effects=True),
    )(block_len, target, queries, keys, values, cotangent, out_weight)
    embedding, grad = pl.pallas_call(
        settle,
        out_shape=(
            jax.ShapeDtypeStruct(cotangent.shape, BF16),
            jax.ShapeDtypeStruct((shard, width), F32),
        ),
        in_specs=[vmem] * 3,
        out_specs=(vmem, vmem),
    )(embedding, rows_sum, factor)
    if not finish:
        lines = [[i for i in range(n_dp) if i % group == g] for g in range(group)]
        grad = lax.psum(grad, "dp", axis_index_groups=lines)
        squares = lax.psum(jnp.sum(grad * grad), "fsdp")
        grad = grad * jnp.minimum(1.0, float(width) / jnp.sqrt(squares + 1e-06))
    return embedding, grad


def solution(mesh):
    n_dp, n_fs = mesh.shape["dp"], mesh.shape["fsdp"]
    group = math.gcd(n_dp, 4)
    both = P(("dp", "fsdp"), None, None)
    flat = P(("dp", "fsdp"))
    return jax.shard_map(
        functools.partial(local, n_dp, n_fs, group),
        mesh=mesh,
        in_specs=(both, both, both, flat, flat, both, P("fsdp", None)),
        out_specs=(both, P("fsdp", None)),
        check_vma=False,
    )
```

```python
import functools
import math

import jax
import jax.numpy as jnp
from jax import lax
from jax.experimental import pallas as pl
from jax.experimental.pallas import tpu as pltpu
from jax.sharding import PartitionSpec as P

HEADS = 16
LANES = 128
MESH = pl.DeviceIdType.MESH
F32 = jnp.float32
BF16 = jnp.bfloat16


def starts_of(width, group):
    tiles = width // LANES
    window = -(-tiles // group) * LANES
    return window, [min(i * window, width - window) for i in range(group)]


def marks_of(width):
    tiles = width // LANES
    return [tiles * tenths // 10 * LANES for tenths in (0, 4, 7, 9, 10)]


def kernel(
    n_dp, n_fs, group, finish,
    len_ref, tgt_ref, q_ref, k_ref, v_ref, cot_ref, w_ref,
    emb_ref, grad_ref, factor_ref,
    wq, cq, mine, nxt, arr, placed, gpart, yrecv, zsend, zrecv, esend, ebuf, tbuf, sbuf, srecv, gsum,
    wz_s, wz_r, wy_s, wy_r, c_s, c_r, n_s, n_r, p_s, p_r, gy_s, gy_r, gz_s, gz_r,
    e_s, e_r, t_s, t_r, q_s, q_r, m_s, m_r,
):
    slots, rows, width = q_ref.shape
    shard = w_ref.shape[0]
    hd = width // HEADS
    window, starts = starts_of(width, group)
    over = group * window - width
    nz = n_fs // 2
    d, f = lax.axis_index("dp"), lax.axis_index("fsdp")
    base = (d // group) * group
    gi = d - base
    z, y = f // 2, f % 2
    other = z * 2 + (1 - y)
    ahead, behind = (d + 1) % n_dp, (d + n_dp - 1) % n_dp
    mates = [(gi + j) % group for j in range(1, group)]
    core, side = gi % 2, gi // 2
    partner, across = side * 2 + (1 - core), (1 - side) * 2 + core

    def start_of(i):
        if group == 1:
            return 0
        return pl.multiple_of(i * window - (i // (group - 1)) * over, LANES)

    def copy(src, dst, s, r, to):
        return pltpu.make_async_remote_copy(
            src_ref=src, dst_ref=dst, send_sem=s, recv_sem=r, device_id=to, device_id_type=MESH
        )

    def spread(at, s, r):
        to = [partner, across] if group == 4 else mates
        made = [copy(at(gi), at(gi), s(j), r(j), (base + m, f)) for j, m in enumerate(to)]
        for c in made:
            c.start()
        return made

    def relay(made, at, s, r):
        if group != 4:
            return made
        made[1].wait_recv()
        c = copy(at(across), at(across), s(2), r(2), (base + partner, f))
        c.start()
        made.append(c)
        return [made[0], c]

    barrier = pltpu.get_barrier_semaphore()
    peers = [(ahead, f), (behind, f)]
    peers += [(base + m, f) for m in mates]
    peers += [(d, (f + j) % n_fs) for j in range(1, n_fs)]
    for peer in peers:
        pl.semaphore_signal(barrier, inc=1, device_id=peer, device_id_type=MESH)

    my_cols = pl.ds(start_of(gi), window)
    my_rows = pl.ds(pl.multiple_of(gi * rows, rows), rows)

    def w_at(index):
        return wq.at[pl.ds(pl.multiple_of(index * shard, shard), shard), :]

    wz, wy, cots = [], [], []

    def open_links():
        pl.semaphore_wait(barrier, len(peers))
        w_src = w_ref.at[:, my_cols]
        for j in range(1, nz):
            c = copy(w_src, w_at(f), wz_s.at[j], wz_r.at[j], (d, ((z + j) % nz) * 2 + y))
            c.start()
            wz.append(c)
        wy.append(copy(w_src, w_at(f), wy_s.at[0], wy_r.at[0], (d, other)))
        wy[0].start()
        for j, m in enumerate(mates):
            c = copy(
                cot_ref.at[0, :, pl.ds(start_of(m), window)], cq.at[my_rows, :],
                c_s.at[j], c_r.at[j], (base + m, f),
            )
            c.start()
            cots.append(c)
        wq[pl.ds(pl.multiple_of(f * shard, shard), shard), :] = w_ref[:, my_cols]
        cq[my_rows, :] = cot_ref[0, :, my_cols]

    key_pos = lax.broadcasted_iota(jnp.int32, (rows, rows), 1)
    row_pos = lax.broadcasted_iota(jnp.int32, (rows, LANES), 0)
    lens = [len_ref[s] for s in range(slots)]
    usable = [key_pos < lens[s] for s in range(slots)]
    limit = [[jnp.where(tgt_ref[s] == t, lens[s], 0) for s in range(slots)] for t in range(2)]
    keep = [[row_pos < limit[t][s] for s in range(slots)] for t in range(2)]
    tiles = {}
    marks = marks_of(width)
    parts = len(marks) - 1
    nexts, cast_all = [], []

    def send_next(part):
        cols = pl.ds(marks[part], marks[part + 1] - marks[part])
        c = copy(nxt.at[:, cols], arr.at[:, cols], n_s.at[part], n_r.at[part], (ahead, f))
        c.start()
        nexts.append(c)

    def placed_at(part):
        cols = pl.ds(marks[part], marks[part + 1] - marks[part])
        return lambda i: placed.at[pl.ds(pl.multiple_of(i * rows, rows), rows), cols]

    def cast(part):
        nexts[part].wait_recv()
        cols = pl.ds(marks[part], marks[part + 1] - marks[part])
        placed[my_rows, cols] = mine[:, cols] + arr[:, cols]
        return spread(placed_at(part), lambda j: p_s.at[part, j], lambda j: p_r.at[part, j])

    def hand_on(part, made):
        return relay(
            made, placed_at(part), lambda j: p_s.at[part, j], lambda j: p_r.at[part, j]
        )

    for h in range(HEADS):
        first, last = h * hd, (h + 1) * hd
        lo, hi = first // LANES * LANES, -(-last // LANES) * LANES
        lane = lax.broadcasted_iota(jnp.int32, (rows, hi - lo), 1) + lo
        inside = (lane >= first) & (lane < last)
        for s in range(slots):
            query = jnp.where(inside, q_ref[s, :, lo:hi].astype(F32), 0.0).astype(BF16)
            scores = lax.dot_general(
                query, k_ref[s, :, lo:hi], (((1,), (1,)), ((), ())), preferred_element_type=F32
            ) * hd ** (-0.5)
            scores = jnp.where(usable[s], scores, -1e30)
            exponent = jnp.exp(scores - jnp.max(scores, axis=-1, keepdims=True))
            weights = (exponent / jnp.sum(exponent, axis=-1, keepdims=True)).astype(BF16)
            mixed = jnp.dot(weights, v_ref[s, :, lo:hi], preferred_element_type=F32)
            mixed = jnp.where(inside, mixed, 0.0)
            for t in range(lo // LANES, hi // LANES):
                piece = mixed[:, t * LANES - lo:(t + 1) * LANES - lo]
                tiles[s, t] = tiles[s, t] + piece if (s, t) in tiles else piece
        for t in range(lo // LANES, hi // LANES):
            if (t + 1) * LANES <= last:
                cols = slice(t * LANES, (t + 1) * LANES)
                for dest, ref in ((0, mine), (1, nxt)):
                    total = sum(
                        jnp.where(keep[dest][s], tiles[s, t], 0.0) for s in range(slots)
                    )
                    ref[:, cols] = total.astype(BF16)
        if h == HEADS // 8 - 1:
            open_links()
        ready = last // LANES * LANES
        while len(nexts) < parts - 1 and marks[len(nexts) + 1] <= ready:
            send_next(len(nexts))
            if len(nexts) > 1:
                cast_all.append(cast(len(nexts) - 2))
    send_next(parts - 1)
    cast_all.append(cast(parts - 2))
    waits = hand_on(0, cast_all[0])
    cast_all.append(cast(parts - 1))
    for j in range(1, nz):
        wz[j - 1].wait_recv()
        from_f = ((z + nz - j) % nz) * 2 + y
        c = copy(w_at(from_f), w_at(from_f), wy_s.at[j], wy_r.at[j], (d, other))
        c.start()
        wy.append(c)

    for part in range(1, parts):
        waits += hand_on(part, cast_all[part])
    casts = sum(cast_all, [])
    for c in cots + waits:
        c.wait_recv()

    step = 2 * LANES
    for i in range(width // step):
        gpart[i * step:(i + 1) * step, :] = lax.dot_general(
            placed[:, i * step:(i + 1) * step], cq[...], (((0,), (0,)), ((), ())),
            preferred_element_type=F32,
        ).astype(BF16)

    def g_rows(index):
        return pl.ds(pl.multiple_of(index * shard, shard), shard)

    order = sorted(range(1, nz), key=lambda j: abs(2 * j - nz)) + [0]
    gy = []
    for j in order:
        zj = (z + j) % nz
        c = copy(
            gpart.at[g_rows(zj * 2 + (1 - y)), :], yrecv.at[zj],
            gy_s.at[j], gy_r.at[j], (d, other),
        )
        c.start()
        gy.append(c)
    gz = []
    for j, c in zip(order, gy):
        zj = (z + j) % nz
        c.wait_recv()
        pair = gpart[g_rows(zj * 2 + y), :].astype(F32) + yrecv[zj].astype(F32)
        if j == 0:
            own = pair
        else:
            zsend[j] = pair.astype(BF16)
            c = copy(zsend.at[j], zrecv.at[j], gz_s.at[j], gz_r.at[j], (d, zj * 2 + y))
            c.start()
            gz.append(c)

    for c in wy:
        c.wait_recv()
    embs = []
    for i in range(group):
        esend[i] = jnp.dot(
            placed[i * rows:(i + 1) * rows, :], wq[...], preferred_element_type=F32
        ).astype(BF16)
    for j, m in enumerate(mates):
        c = copy(esend.at[m], ebuf.at[gi], e_s.at[j], e_r.at[j], (base + m, f))
        c.start()
        embs.append(c)
    ebuf[gi] = esend[gi]

    for c in gz:
        c.wait_recv()
    for j in range(1, nz):
        own = own + zrecv[j].astype(F32)
    ends = starts[1:] + [width]
    tbuf[gi] = own.astype(BF16)
    turn_at = lambda i: tbuf.at[i]
    turn_s, turn_r = (lambda j: t_s.at[j]), (lambda j: t_r.at[j])
    turns = spread(turn_at, turn_s, turn_r)
    squares = []
    if finish:
        valid = window
        for i in range(group):
            valid = jnp.where(gi == i, ends[i] - starts[i], valid)
        lane = lax.broadcasted_iota(jnp.int32, (8, LANES), 1)
        total = jnp.zeros((8, LANES), F32)
        for col in range(0, window, LANES):
            tile = own[:, col:col + LANES].astype(BF16).astype(F32)
            part = jnp.sum((tile * tile).reshape(shard // 8, 8, LANES), axis=0)
            total = total + jnp.where(lane + col < valid, part, 0.0)
        sbuf[...] = total
        for j in range(1, n_fs):
            c = copy(sbuf, srecv.at[j], q_s.at[j], q_r.at[j], (d, (f + j) % n_fs))
            c.start()
            squares.append(c)
    waits = relay(turns, turn_at, turn_s, turn_r)
    if finish:
        for j, c in zip(range(1, n_fs), squares):
            c.wait_recv()
            total = total + srecv[j]
        gsum[gi] = total
        for j, m in enumerate(mates):
            c = copy(gsum.at[gi], gsum.at[gi], m_s.at[j], m_r.at[j], (base + m, f))
            c.start()
            squares.append(c)
    for c in embs:
        c.wait_recv()
    for i in range(group):
        emb_ref[0, :, starts[i]:ends[i]] = ebuf[i, :, 0:ends[i] - starts[i]]
    for c in waits:
        c.wait_recv()
    if finish:
        for c in squares[n_fs - 1:]:
            c.wait_recv()
        total = gsum[0]
        for i in range(1, group):
            total = total + gsum[i]
        norm = jnp.sqrt(jnp.sum(total, keepdims=True) + 1e-06)
        factor = jnp.minimum(1.0, float(width) / norm)
    for i in range(group):
        grad_ref[:, starts[i]:ends[i]] = tbuf[i, :, 0:ends[i] - starts[i]]
    factor_ref[...] = jnp.broadcast_to(factor, factor_ref.shape) if finish else jnp.ones_like(factor_ref)
    for c in wz + wy + cots + nexts + casts + gy + gz + embs + turns + squares:
        c.wait_send()


def settle(emb_ref, rows_ref, factor_ref, emb_out, grad_out):
    emb_out[...] = emb_ref[...]
    grad_out[...] = rows_ref[...].astype(F32) * factor_ref[0:1, 0:1]


def local(n_dp, n_fs, group, queries, keys, values, block_len, target, cotangent, out_weight):
    slots, rows, width = queries.shape
    shard = out_weight.shape[0]
    window, starts = starts_of(width, group)
    nz = n_fs // 2
    finish = group == n_dp
    vmem = pl.BlockSpec(memory_space=pltpu.VMEM)
    smem = pl.BlockSpec(memory_space=pltpu.SMEM)
    sem = lambda *shape: pltpu.SemaphoreType.DMA(shape)
    mates = max(group - 1, 1)
    parts = len(marks_of(width)) - 1
    embedding, rows_sum, factor = pl.pallas_call(
        functools.partial(kernel, n_dp, n_fs, group, finish),
        out_shape=(
            jax.ShapeDtypeStruct(cotangent.shape, BF16),
            jax.ShapeDtypeStruct((shard, width), BF16),
            jax.ShapeDtypeStruct((8, LANES), F32),
        ),
        in_specs=[smem, smem] + [vmem] * 5,
        out_specs=(vmem, vmem, vmem),
        scratch_shapes=[
            pltpu.VMEM((width, window), BF16),
            pltpu.VMEM((group * rows, window), BF16),
            pltpu.VMEM((rows, width), BF16),
            pltpu.VMEM((rows, width), BF16),
            pltpu.VMEM((rows, width), BF16),
            pltpu.VMEM((group * rows, width), BF16),
            pltpu.VMEM((width, window), BF16),
            pltpu.VMEM((nz, shard, window), BF16),
            pltpu.VMEM((nz, shard, window), BF16),
            pltpu.VMEM((nz, shard, window), BF16),
            pltpu.VMEM((group, rows, window), BF16),
            pltpu.VMEM((group, rows, window), BF16),
            pltpu.VMEM((group, shard, window), BF16),
            pltpu.VMEM((8, LANES), F32),
            pltpu.VMEM((n_fs, 8, LANES), F32),
            pltpu.VMEM((group, 8, LANES), F32),
            sem(nz), sem(nz), sem(nz), sem(nz), sem(mates), sem(mates), sem(parts), sem(parts),
            sem(parts, mates), sem(parts, mates), sem(nz), sem(nz), sem(nz), sem(nz),
            sem(mates), sem(mates), sem(mates), sem(mates), sem(n_fs), sem(n_fs),
            sem(mates), sem(mates),
        ],
        compiler_params=pltpu.CompilerParams(collective_id=0, has_side_effects=True),
    )(block_len, target, queries, keys, values, cotangent, out_weight)
    embedding, grad = pl.pallas_call(
        settle,
        out_shape=(
            jax.ShapeDtypeStruct(cotangent.shape, BF16),
            jax.ShapeDtypeStruct((shard, width), F32),
        ),
        in_specs=[vmem] * 3,
        out_specs=(vmem, vmem),
    )(embedding, rows_sum, factor)
    if not finish:
        lines = [[i for i in range(n_dp) if i % group == g] for g in range(group)]
        grad = lax.psum(grad, "dp", axis_index_groups=lines)
        squares = lax.psum(jnp.sum(grad * grad), "fsdp")
        grad = grad * jnp.minimum(1.0, float(width) / jnp.sqrt(squares + 1e-06))
    return embedding, grad


def solution(mesh):
    n_dp, n_fs = mesh.shape["dp"], mesh.shape["fsdp"]
    group = math.gcd(n_dp, 4)
    both = P(("dp", "fsdp"), None, None)
    flat = P(("dp", "fsdp"))
    return jax.shard_map(
        functools.partial(local, n_dp, n_fs, group),
        mesh=mesh,
        in_specs=(both, both, both, flat, flat, both, P("fsdp", None)),
        out_specs=(both, P("fsdp", None)),
        check_vma=False,
    )
```
